32 devices in a mesh: grp: 4 (over y, x), dom: 8 (over z, core).
Axes of the slice: x: 2, y: 2, z: 4, core: 2. Of those that a mesh axis runs over, the one named last changes fastest.
Arguments:
- displacement: float32 [4, 3, 16, 96, 128], P('grp', None, 'dom'), may hold values from -3 to 3
- velocity: float32 [4, 3, 16, 96, 128], P('grp', None, 'dom'), may hold values from -6 to 6
- external: float32 [4, 3, 16, 96, 128], P('grp', None, 'dom'), may hold values from -6 to 6
- mass: float32 [4, 16, 96, 128], P('grp', 'dom'), may hold values from 1 to 3
- elem_scale: float32 [4, 16, 96, 128], P('grp', 'dom'), may hold values from 0.05 to 0.5
- stiffness: float32 [4, 24, 24], P('grp'), as said below
- substeps: int32 [4], P('grp'), may hold values from 1 to 8
- own_nodes: int32 [4, 128], P('grp', 'dom'), may hold values from 0 to 24575, as said below
- peer_nodes: int32 [4, 128], P('grp', 'dom'), may hold values from 0 to 24575, as said below
- normals: float32 [4, 3, 128], P('grp', None, 'dom'), may hold values from -4 to 4
- schur_inverse: float32 [512, 512], P(('grp', 'dom')), as said below
Outputs:
- new_displacement: float32 [4, 3, 16, 96, 128], P('grp', None, 'dom')
- new_velocity: float32 [4, 3, 16, 96, 128], P('grp', None, 'dom')
The draws below stay inside these ranges and needn't reach their ends.
Inputs may be any that keep to these rules, and one draw needn't show every extreme that they name: `own_nodes`: the 16 entries of one device's block are distinct. `peer_nodes`: the 16 entries of one device's block are distinct. `schur_inverse`: symmetric. `stiffness`: symmetric positive definite.
All inputs are finite; a program needn't handle non-finite values.
Results may differ from the reference program's by a relative error of at most 0.0001.
Values sent between devices are 32-bit elements; how exact they have to be, the bound alone decides.
A program may use at most 64 MiB of HBM per device.

```python
import math
import jax
import jax.numpy as jnp
from jax import lax

SY = 96
SZ = 128
IF_DEV = 16
MAXSUB = 8
GROUPS = 4
NX = 16
NODES_DEV = 24576
IFACE = 128
LAM = 512
N_DOM = 8


def draw_stiffness(key, part):
    base = jax.random.normal(jax.random.fold_in(key, 5), (GROUPS, 24, 24), jnp.float32) / math.sqrt(24.0)
    return jnp.einsum('gik,gjk->gij', base, base)


def pick_nodes(key, salt):
    keys = jax.random.split(jax.random.fold_in(key, salt), GROUPS * N_DOM)

    def single(one_key):
        return jax.random.permutation(one_key, NODES_DEV)[:IF_DEV]
    picks = jax.vmap(single)(keys)
    return picks.reshape(GROUPS, IFACE).astype(jnp.int32)


def draw_own_nodes(key, part):
    return pick_nodes(key, 11)


def draw_peer_nodes(key, part):
    return pick_nodes(key, 23)


def draw_schur_inverse(key, part):
    base = jax.random.normal(jax.random.fold_in(key, 1), (LAM, LAM), jnp.float32) * (0.5 / math.sqrt(LAM))
    sym = (base + base.T) * 0.5
    diag = jnp.exp(jax.random.uniform(jax.random.fold_in(key, 2), (LAM,), jnp.float32, math.log(0.5), math.log(2.0)))
    return sym + jnp.diag(diag)


def with_ends(entries, key, smallest, largest):
    place = [jax.random.randint(jax.random.fold_in(key, axis), (), 0, length) for axis, length in enumerate(entries.shape)]
    widest = entries.shape.index(max(entries.shape))
    neighbour = place[:widest] + [(place[widest] + 1) % entries.shape[widest]] + place[widest + 1:]
    return entries.at[tuple(place)].set(smallest).at[tuple(neighbour)].set(largest)


def steps_of(key, shape, cuts, low, high):
    level = 1.0
    for dim, shards_of in cuts:
        heights = jax.random.uniform(jax.random.fold_in(jax.random.fold_in(key, 6), dim), (shards_of,), jnp.float32, low / len(cuts), high / len(cuts))
        level = level * jnp.repeat(jnp.exp(heights), shape[dim] // shards_of).reshape((-1,) + (1,) * (len(shape) - 1 - dim))
    return level


def scatter_about(key, extent, scale, reach, cuts=(), kind=jnp.bfloat16):
    level = steps_of(key, extent, cuts, -0.22, 0.18) if cuts else 1.0
    entries = jax.random.normal(key, extent, jnp.float32) * scale * level
    return jnp.minimum(jnp.maximum(entries, -reach), reach).astype(kind)


def setup_inputs(seed: int = 0) -> dict:
    streams_of = jax.random.split(jax.random.key(seed), 12)
    displacement = scatter_about(streams_of[0], (GROUPS, 3, NX, SY, SZ), 0.5, 3.0, ((0, 4), (2, 8)), jnp.float32)
    velocity = scatter_about(streams_of[1], (GROUPS, 3, NX, SY, SZ), 1.0, 6.0, ((0, 4), (2, 8)), jnp.float32)
    external = scatter_about(streams_of[2], (GROUPS, 3, NX, SY, SZ), 1.0, 6.0, ((0, 4), (2, 8)), jnp.float32)
    mass = jnp.clip(jnp.exp(math.log(3.0) - 1.0986123 * jax.random.uniform(streams_of[3], (GROUPS, NX, SY, SZ), jnp.float32) ** steps_of(streams_of[3], (GROUPS, NX, SY, SZ), ((0, 4), (1, 8)), -0.2, 0.2)), 1.0, 3.0)
    elem_scale = jnp.clip(jnp.exp(math.log(0.5) - 2.3025851 * jax.random.uniform(streams_of[4], (GROUPS, NX, SY, SZ), jnp.float32) ** steps_of(streams_of[4], (GROUPS, NX, SY, SZ), ((0, 4), (1, 8)), -0.2, 0.2)), 0.05, 0.5)
    stiffness = draw_stiffness(jax.random.fold_in(streams_of[11], 71), 0)
    substeps = with_ends(jax.random.randint(streams_of[6], (GROUPS,), 1, MAXSUB + 1), jax.random.fold_in(streams_of[6], 1), 1, MAXSUB).astype(jnp.int32)
    own_nodes = draw_own_nodes(jax.random.fold_in(streams_of[11], 71), 0)
    peer_nodes = draw_peer_nodes(jax.random.fold_in(streams_of[11], 71), 0)
    normals = scatter_about(streams_of[9], (GROUPS, 3, IFACE), 1.0, 4.0, ((0, 4), (2, 8)), jnp.float32)
    schur_inverse = draw_schur_inverse(jax.random.fold_in(streams_of[11], 71), 0)
    return dict(displacement=displacement, velocity=velocity, external=external, mass=mass, elem_scale=elem_scale, stiffness=stiffness, substeps=substeps, own_nodes=own_nodes, peer_nodes=peer_nodes, normals=normals, schur_inverse=schur_inverse)


coarse_step = 0.4


def corner_stack(padded, planes):
    pieces = []
    for plane_off in (0, 1):
        for row_off in (0, 1):
            for col_off in (0, 1):
                block = padded[:, plane_off:plane_off + planes]
                block = jnp.roll(block, -row_off, axis=2)
                pieces.append(jnp.roll(block, -col_off, axis=3))
    return jnp.stack(pieces, 0).reshape(24, -1)


def element_forces(padded, scale, kmat):
    stacked = corner_stack(padded, scale.shape[0])
    forces = jnp.dot(kmat, stacked, precision=lax.Precision.HIGHEST, preferred_element_type=jnp.float32)
    forces = forces * scale.reshape(1, -1)
    return forces.reshape((8, 3) + scale.shape)


def assemble(forces):
    planes = forces.shape[2]
    total = jnp.zeros((3, planes + 1) + forces.shape[3:], jnp.float32)
    corner = 0
    for plane_off in (0, 1):
        for row_off in (0, 1):
            for col_off in (0, 1):
                part = jnp.roll(jnp.roll(forces[corner], row_off, axis=2), col_off, axis=3)
                total = total + jnp.pad(part, ((0, 0), (plane_off, 1 - plane_off), (0, 0), (0, 0)))
                corner = corner + 1
    return total


def group_internal(field, scale, kmat):
    padded = jnp.concatenate([field, jnp.zeros_like(field[:, :1])], 1)
    return assemble(element_forces(padded, scale, kmat))[:, :-1]


def reference(displacement, velocity, external, mass, elem_scale, stiffness, substeps, own_nodes, peer_nodes, normals, schur_inverse):
    fields = []
    speeds = []
    for group in range(GROUPS):
        delta = coarse_step / substeps[group].astype(jnp.float32)
        loads = external[group]
        weight = mass[group]
        scale = elem_scale[group]
        kmat = stiffness[group]

        def advance(step, state, loads=loads, weight=weight, scale=scale, kmat=kmat, delta=delta):
            field, speed = state
            accel = (loads - group_internal(field, scale, kmat)) / weight
            speed = speed + delta * accel
            field = field + delta * speed
            return field, speed

        field, speed = lax.fori_loop(0, substeps[group], advance, (displacement[group], velocity[group]))
        fields.append(field)
        speeds.append(speed.reshape(3, -1))
    offsets = (jnp.arange(N_DOM, dtype=jnp.int32) * NODES_DEV)[:, None]
    own_global = [(own_nodes[g].reshape(N_DOM, IF_DEV) + offsets).reshape(-1) for g in range(GROUPS)]
    peer_global = [(peer_nodes[g].reshape(N_DOM, IF_DEV) + offsets).reshape(-1) for g in range(GROUPS)]
    gaps = []
    for group in range(GROUPS):
        later = (group + 1) % GROUPS
        diff = speeds[group][:, own_global[group]] - speeds[later][:, peer_global[later]]
        gaps.append(jnp.sum(normals[group] * diff, axis=0))
    gap = jnp.concatenate(gaps, 0)
    multiplier = jnp.dot(schur_inverse, gap, precision=lax.Precision.HIGHEST, preferred_element_type=jnp.float32)
    multiplier = multiplier.reshape(GROUPS, IFACE)
    results = []
    for group in range(GROUPS):
        earlier = (group - 1) % GROUPS
        masses = mass[group].reshape(-1)
        correction = multiplier[group][None, :] * normals[group]
        incoming = multiplier[earlier][None, :] * normals[earlier]
        speed = speeds[group]
        speed = speed.at[:, own_global[group]].add(-correction / masses[own_global[group]][None, :])
        speed = speed.at[:, peer_global[group]].add(incoming / masses[peer_global[group]][None, :])
        results.append(speed.reshape(3, NX, SY, SZ))
    return jnp.stack(fields, 0), jnp.stack(results, 0)
```

```python
import functools

import jax
import jax.numpy as jnp
from jax import lax
from jax.experimental import pallas as pl
from jax.experimental.pallas import tpu as pltpu
from jax.sharding import PartitionSpec as P

MAXSUB = 8
MESH = pl.DeviceIdType.MESH
HIGH = lax.Precision.HIGHEST
F32 = jnp.float32
BF16 = jnp.bfloat16

coarse_step = 0.4

BLOCK = 8
WINDOW = 16
OUT_HALF = 12 * BLOCK
IN_HALF = 6 * WINDOW


def iota(shape, dim):
    return lax.broadcasted_iota(jnp.int32, shape, dim)


def halves(x):
    high = x.astype(BF16)
    return high, (x - high.astype(F32)).astype(BF16)


def block_matrix(kmat):
    outs, ins = 2 * OUT_HALF, 2 * IN_HALF

    def out_parts(q):
        a = (q >= OUT_HALF).astype(jnp.int32)
        q = q - a * OUT_HALF
        b = (q >= OUT_HALF // 2).astype(jnp.int32)
        q = q - b * (OUT_HALF // 2)
        return a, b, q >> 4, (q >> 3) & 1, q & 7

    def in_parts(q):
        a = (q >= IN_HALF).astype(jnp.int32)
        q = q - a * IN_HALF
        return a, q >> 5, (q >> 4) & 1, q & 15

    a, b, comp, e, _ = out_parts(iota((outs, 24), 0))
    pick = (iota((outs, 24), 1) == 3 * (4 * a + 2 * b + e) + comp).astype(F32)
    left = jnp.dot(pick, kmat, precision=HIGH, preferred_element_type=F32)
    row = out_parts(iota((outs, ins), 0))[4]
    window_row = in_parts(iota((outs, ins), 1))[3]
    total = jnp.zeros((outs, ins), F32)
    a, comp, e, _ = in_parts(iota((24, ins), 1))
    for b in (0, 1):
        place = (iota((24, ins), 0) == 3 * (4 * a + 2 * b + e) + comp).astype(F32)
        spread = jnp.dot(left, place, precision=HIGH, preferred_element_type=F32)
        total = jnp.where(window_row - row == b, spread, total)
    return total


def kernel(
    dims, disp, vel, ext, mass, scale, stiff, sub, own, peer, norm, schur,
    o_u, o_v,
    split_hi, split_lo, force, halo, scale_low, minv, amat, norm_own, norm_prev, schur_prev,
    parts, picked, w_gap, w_fix, hot,
    halo_send, halo_recv, init_send, init_recv, part_send, part_recv,
):
    n_grp, n_dom, planes, ny, nz, n_if = dims
    g, d = lax.axis_index("grp"), lax.axis_index("dom")
    n_dev = n_grp * n_dom
    me = g * n_dom + d
    n_pair = ny // WINDOW

    barrier = pltpu.get_barrier_semaphore()

    def greet(k, carry):
        to = lax.rem(me + k, n_dev)
        pl.semaphore_signal(
            barrier, inc=1, device_id=(to // n_dom, lax.rem(to, n_dom)), device_id_type=MESH
        )
        return carry

    lax.fori_loop(1, n_dev, greet, 0)

    def split_store(x, plane, comp):
        for e in (0, 1):
            y = x if e == 0 else pltpu.roll(x, nz - 1, 1)
            high, low = halves(y)
            turned = jnp.concatenate([y[BLOCK:], y[:BLOCK]], 0)
            high2, low2 = halves(turned)
            at = pl.ds(plane * IN_HALF + (comp * 2 + e) * WINDOW, WINDOW)
            for p in range(n_pair):
                cut = slice(p * WINDOW, (p + 1) * WINDOW)
                split_hi[p, at, :nz] = high[cut]
                split_hi[p, at, nz:] = high2[cut]
                split_lo[p, at, :nz] = low[cut]
                split_lo[p, at, nz:] = low2[cut]

    norm_own[...] = jnp.zeros_like(norm_own)
    norm_own[0:3, 0:n_if] = norm[...]
    o_u[...] = disp[...]
    o_v[...] = vel[...]
    minv[...] = 1.0 / mass[...]

    @pl.when(d == 0)
    def _():
        scale_low[...] = jnp.zeros_like(scale_low)
        for slot in (0, 1):
            halo[slot, 0] = jnp.zeros((3, ny, nz), F32)

    @pl.when(d == n_dom - 1)
    def _():
        for slot in (0, 1):
            halo[slot, 1] = jnp.zeros((3, ny, nz), F32)

    def to_prev(src, slot):
        return pltpu.make_async_remote_copy(
            src_ref=src.at[:, pl.ds(0, ny), :],
            dst_ref=halo.at[slot, 1],
            send_sem=halo_send.at[0],
            recv_sem=halo_recv.at[slot, 1],
            device_id=(g, d - 1),
            device_id_type=MESH,
        )

    def to_next(src, slot):
        return pltpu.make_async_remote_copy(
            src_ref=src.at[:, pl.ds((planes - 1) * ny, ny), :],
            dst_ref=halo.at[slot, 0],
            send_sem=halo_send.at[1],
            recv_sem=halo_recv.at[slot, 0],
            device_id=(g, d + 1),
            device_id_type=MESH,
        )

    scale_copy = pltpu.make_async_remote_copy(
        src_ref=scale.at[pl.ds((planes - 1) * ny, ny), :],
        dst_ref=scale_low,
        send_sem=init_send.at[0],
        recv_sem=init_recv.at[0],
        device_id=(g, d + 1),
        device_id_type=MESH,
    )
    later = (lax.rem(g + 1, n_grp), d)
    norm_copy = pltpu.make_async_remote_copy(
        src_ref=norm_own,
        dst_ref=norm_prev,
        send_sem=init_send.at[1],
        recv_sem=init_recv.at[1],
        device_id=later,
        device_id_type=MESH,
    )
    schur_copy = pltpu.make_async_remote_copy(
        src_ref=schur,
        dst_ref=schur_prev,
        send_sem=init_send.at[2],
        recv_sem=init_recv.at[2],
        device_id=later,
        device_id_type=MESH,
    )

    pl.semaphore_wait(barrier, n_dev - 1)

    @pl.when(d > 0)
    def _():
        to_prev(o_u, 0).start()

    @pl.when(d < n_dom - 1)
    def _():
        to_next(o_u, 0).start()
        scale_copy.start()

    norm_copy.start()
    schur_copy.start()

    high, low = halves(block_matrix(stiff[...]))
    amat[:, 0 : 2 * IN_HALF] = high
    amat[:, 2 * IN_HALF : 4 * IN_HALF] = high
    amat[:, 4 * IN_HALF : 6 * IN_HALF] = low
    for plane in range(planes):
        for comp in range(3):
            split_store(disp[comp, plane * ny : (plane + 1) * ny, :], plane + 1, comp)

    two = 2 * n_if
    nodes = [own[0, i] for i in range(n_if)] + [peer[0, i] for i in range(n_if)]
    node_rows = [node // nz for node in nodes]

    def layer(index, corners, seen):
        first = min(corners) * OUT_HALF
        weights = amat[first : first + len(corners) * OUT_HALF, :]
        for p in range(n_pair):
            rows_in = pl.ds(index * IN_HALF, 2 * IN_HALF)
            top = split_hi[p, rows_in, :]
            stacked = jnp.concatenate([top, split_lo[p, rows_in, :], top], 0)
            result = jnp.dot(weights, stacked, preferred_element_type=F32)
            for half in (0, 1):
                start = (2 * p + half) * BLOCK
                if index == 0:
                    factor = scale_low[start : start + BLOCK, :]
                else:
                    at = (index - 1) * ny + start
                    factor = scale[at : at + BLOCK, :]
                lanes = slice(half * nz, (half + 1) * nz)
                for k, a in enumerate(corners):
                    plane = index - 1 + a
                    for b in (0, 1):
                        for comp in range(3):
                            base = k * OUT_HALF + b * (OUT_HALF // 2) + comp * WINDOW
                            near = result[base : base + BLOCK, lanes] * factor
                            far = result[base + BLOCK : base + WINDOW, lanes] * factor
                            part = near + pltpu.roll(far, 1, 1)
                            at = pl.ds(plane * ny + start, BLOCK)
                            if plane in seen:
                                part = part + force[b, comp, at, :]
                            force[b, comp, at, :] = part
        for a in corners:
            seen.add(index - 1 + a)

    count = jnp.full((1, nz), sub[0], jnp.int32)
    full_delta = coarse_step / count.astype(F32)

    def prepare():
        norm_copy.wait_recv()
        schur_copy.wait_recv()
        lane = iota((two, nz), 1)
        row = iota((two, nz), 0)
        columns = jnp.zeros((two, nz), jnp.int32)
        wide = iota((1, 3 * two), 1)
        rows = jnp.zeros((1, 3 * two), jnp.int32)
        for i in range(two):
            columns = jnp.where(row == i, nodes[i] - node_rows[i] * nz, columns)
            for rep in range(3):
                rows = jnp.where(wide == rep * two + i, node_rows[i], rows)
            picked[0, i : i + 1, :] = minv[pl.ds(node_rows[i], 1), :]
        at_node = lane == columns
        size = planes * ny
        hot[...] = (iota((size, 3 * two), 0) == rows).astype(F32).astype(BF16)
        inverse = picked[0]
        diagonal = iota((n_if, nz), 0) == iota((n_if, nz), 1)
        sign = jnp.where(row < n_if, -1.0, 1.0).astype(F32)
        for comp in range(3):
            cols = []
            for ref in (norm_own, norm_prev):
                spread = jnp.where(diagonal, ref[comp : comp + 1, :], 0.0)
                cols.append(jnp.sum(spread, axis=1, keepdims=True))
            here = jnp.where(at_node, jnp.concatenate(cols, 0), 0.0)
            w_gap[comp] = here
            w_fix[comp] = here * sign * inverse

    def advance(step, carry):
        slot = lax.rem(step, 2)
        seen = set()
        for index in range(1, planes):
            layer(index, (0, 1), seen)

        @pl.when(d > 0)
        def _():
            to_next(o_u, slot).wait_recv()

        @pl.when(d < n_dom - 1)
        def _():
            to_prev(o_u, slot).wait_recv()

        @pl.when((step == 0) & (d > 0))
        def _():
            scale_copy.wait_recv()

        for comp in range(3):
            split_store(halo[slot, 0, comp], 0, comp)
            split_store(halo[slot, 1, comp], planes + 1, comp)
        layer(0, (1,), seen)
        layer(planes, (0,), seen)

        @pl.when(d > 0)
        def _():
            to_prev(o_u, slot).wait_send()

        @pl.when(d < n_dom - 1)
        def _():
            to_next(o_u, slot).wait_send()

        delta = jnp.where(step < count, full_delta, 0.0)
        for plane in range(planes):
            at = slice(plane * ny, (plane + 1) * ny)
            for comp in range(3):
                inner = force[0, comp, at, :] + pltpu.roll(force[1, comp, at, :], 1, 0)
                speed = o_v[comp, at, :] + delta * ((ext[comp, at, :] - inner) * minv[at, :])
                field = o_u[comp, at, :] + delta * speed
                o_v[comp, at, :] = speed
                o_u[comp, at, :] = field
                split_store(field, plane + 1, comp)

        @pl.when((step < MAXSUB - 1) & (d > 0))
        def _():
            to_prev(o_u, 1 - slot).start()

        @pl.when((step < MAXSUB - 1) & (d < n_dom - 1))
        def _():
            to_next(o_u, 1 - slot).start()

        @pl.when(step == 0)
        def _():
            prepare()

        return carry

    lax.fori_loop(0, MAXSUB, advance, 0)

    for comp in range(3):
        for i in range(two):
            picked[comp, i : i + 1, :] = o_v[comp, pl.ds(node_rows[i], 1), :]
    summed = picked[0] * w_gap[0] + picked[1] * w_gap[1] + picked[2] * w_gap[2]
    columns = jnp.sum(summed, axis=1, keepdims=True)
    per_row = nz // n_if
    offset = lax.rem(d, per_row) * n_if
    place = iota((n_if, nz), 1) == iota((n_if, nz), 0) + offset
    for k in (0, 1):
        spread = jnp.where(place, columns[k * n_if : (k + 1) * n_if, :], 0.0)
        parts[me, k : k + 1, :] = jnp.sum(spread, axis=0, keepdims=True)

    def part_copy(to, source):
        return pltpu.make_async_remote_copy(
            src_ref=parts.at[source],
            dst_ref=parts.at[source],
            send_sem=part_send.at[to],
            recv_sem=part_recv.at[source],
            device_id=(to // n_dom, lax.rem(to, n_dom)),
            device_id_type=MESH,
        )

    def send(k, carry):
        part_copy(lax.rem(me + k, n_dev), me).start()
        return carry

    def receive(k, carry):
        source = lax.rem(me + k, n_dev)
        part_copy(source, source).wait_recv()
        return carry

    def finish(k, carry):
        part_copy(lax.rem(me + k, n_dev), me).wait_send()
        return carry

    lax.fori_loop(1, n_dev, send, 0)
    lax.fori_loop(1, n_dev, receive, 0)

    n_rows = n_dom // per_row
    totals = [
        [
            jnp.sum(parts[group * n_dom + k * per_row : group * n_dom + (k + 1) * per_row], axis=0)
            for k in range(n_rows)
        ]
        for group in range(n_grp)
    ]
    mine = jnp.zeros((n_if, nz), F32)
    before = jnp.zeros((n_if, nz), F32)
    for group in range(n_grp):
        for k in range(n_rows):
            gap = totals[group][k][0:1] - totals[(group + 1) % n_grp][k][1:2]
            at = slice((group * n_rows + k) * nz, (group * n_rows + k + 1) * nz)
            mine = mine + schur[:, at] * gap
            before = before + schur_prev[:, at] * gap
    factors = jnp.sum(jnp.concatenate([mine, before], 0), axis=1, keepdims=True)
    fixes = jnp.concatenate([factors * w_fix[comp] for comp in range(3)], 1)
    first, rest = fixes.astype(BF16), fixes
    rest = rest - first.astype(F32)
    second = rest.astype(BF16)
    third = (rest - second.astype(F32)).astype(BF16)
    change = jnp.dot(
        hot[...], jnp.concatenate([first, second, third], 0), preferred_element_type=F32
    )
    for comp in range(3):
        o_v[comp] = o_v[comp] + change[:, comp * nz : (comp + 1) * nz]

    lax.fori_loop(1, n_dev, finish, 0)
    norm_copy.wait_send()
    schur_copy.wait_send()

    @pl.when(d < n_dom - 1)
    def _():
        scale_copy.wait_send()


def solution(mesh):
    n_grp, n_dom = mesh.shape["grp"], mesh.shape["dom"]

    def on_device(
        displacement, velocity, external, mass, elem_scale, stiffness,
        substeps, own_nodes, peer_nodes, normals, schur_inverse,
    ):
        _, _, planes, ny, nz = displacement.shape
        n_if = own_nodes.shape[1]
        n_dev = n_grp * n_dom
        n_lam = schur_inverse.shape[1]
        rows = planes * ny
        field = jax.ShapeDtypeStruct((3, rows, nz), F32)
        vmem = pl.BlockSpec(memory_space=pltpu.VMEM)
        smem = pl.BlockSpec(memory_space=pltpu.SMEM)
        new_u, new_v = pl.pallas_call(
            functools.partial(kernel, (n_grp, n_dom, planes, ny, nz, n_if)),
            out_shape=(field, field),
            in_specs=[vmem] * 6 + [smem] * 3 + [vmem] * 2,
            out_specs=(vmem, vmem),
            scratch_shapes=[
                pltpu.VMEM((ny // WINDOW, (planes + 2) * IN_HALF, 2 * nz), BF16),
                pltpu.VMEM((ny // WINDOW, (planes + 2) * IN_HALF, 2 * nz), BF16),
                pltpu.VMEM((2, 3, rows, nz), F32),
                pltpu.VMEM((2, 2, 3, ny, nz), F32),
                pltpu.VMEM((ny, nz), F32),
                pltpu.VMEM((rows, nz), F32),
                pltpu.VMEM((2 * OUT_HALF, 6 * IN_HALF), BF16),
                pltpu.VMEM((8, nz), F32),
                pltpu.VMEM((8, nz), F32),
                pltpu.VMEM((n_if, n_lam), F32),
                pltpu.VMEM((n_dev, 2, nz), F32),
                pltpu.VMEM((3, 2 * n_if, nz), F32),
                pltpu.VMEM((3, 2 * n_if, nz), F32),
                pltpu.VMEM((3, 2 * n_if, nz), F32),
                pltpu.VMEM((rows, 6 * n_if), BF16),
                pltpu.SemaphoreType.DMA((2,)),
                pltpu.SemaphoreType.DMA((2, 2)),
                pltpu.SemaphoreType.DMA((3,)),
                pltpu.SemaphoreType.DMA((3,)),
                pltpu.SemaphoreType.DMA((n_dev,)),
                pltpu.SemaphoreType.DMA((n_dev,)),
            ],
            compiler_params=pltpu.CompilerParams(
                collective_id=0, has_side_effects=True, vmem_limit_bytes=48 << 20
            ),
        )(
            displacement.reshape(3, rows, nz),
            velocity.reshape(3, rows, nz),
            external.reshape(3, rows, nz),
            mass.reshape(rows, nz),
            elem_scale.reshape(rows, nz),
            stiffness[0],
            substeps,
            own_nodes,
            peer_nodes,
            normals[0],
            schur_inverse,
        )
        shape = displacement.shape
        return new_u.reshape(shape), new_v.reshape(shape)

    return jax.shard_map(
        on_device,
        mesh=mesh,
        in_specs=(
            P("grp", None, "dom", None, None),
            P("grp", None, "dom", None, None),
            P("grp", None, "dom", None, None),
            P("grp", "dom", None, None),
            P("grp", "dom", None, None),
            P("grp", None, None),
            P("grp"),
            P("grp", "dom"),
            P("grp", "dom"),
            P("grp", None, "dom"),
            P(("grp", "dom"), None),
        ),
        out_specs=(P("grp", None, "dom", None, None), P("grp", None, "dom", None, None)),
        check_vma=False,
    )
```

```python
import functools

import jax
import jax.numpy as jnp
from jax import lax
from jax.experimental import pallas as pl
from jax.experimental.pallas import tpu as pltpu
from jax.sharding import PartitionSpec as P

MAXSUB = 8
MESH = pl.DeviceIdType.MESH
HIGH = lax.Precision.HIGHEST
F32 = jnp.float32
BF16 = jnp.bfloat16

coarse_step = 0.4

BLOCK = 8
WINDOW = 16
OUT_HALF = 12 * BLOCK
IN_HALF = 6 * WINDOW


def iota(shape, dim):
    return lax.broadcasted_iota(jnp.int32, shape, dim)


def halves(x):
    high = x.astype(BF16)
    return high, (x - high.astype(F32)).astype(BF16)


def block_matrix(kmat):
    outs, ins = 2 * OUT_HALF, 2 * IN_HALF

    def out_parts(q):
        a = (q >= OUT_HALF).astype(jnp.int32)
        q = q - a * OUT_HALF
        b = (q >= OUT_HALF // 2).astype(jnp.int32)
        q = q - b * (OUT_HALF // 2)
        return a, b, q >> 4, (q >> 3) & 1, q & 7

    def in_parts(q):
        a = (q >= IN_HALF).astype(jnp.int32)
        q = q - a * IN_HALF
        return a, q >> 5, (q >> 4) & 1, q & 15

    a, b, comp, e, _ = out_parts(iota((outs, 24), 0))
    pick = (iota((outs, 24), 1) == 3 * (4 * a + 2 * b + e) + comp).astype(F32)
    left = jnp.dot(pick, kmat, precision=HIGH, preferred_element_type=F32)
    row = out_parts(iota((outs, ins), 0))[4]
    window_row = in_parts(iota((outs, ins), 1))[3]
    total = jnp.zeros((outs, ins), F32)
    a, comp, e, _ = in_parts(iota((24, ins), 1))
    for b in (0, 1):
        place = (iota((24, ins), 0) == 3 * (4 * a + 2 * b + e) + comp).astype(F32)
        spread = jnp.dot(left, place, precision=HIGH, preferred_element_type=F32)
        total = jnp.where(window_row - row == b, spread, total)
    return total


def kernel(
    dims, disp, vel, ext_in, mass_in, scale_in, stiff_in, sub_in, own_in, peer_in, norm_in, schur_in,
    o_u, o_v,
    ext, mass, scale, stiff, sub, own, peer, norm, schur,
    split_hi, split_lo, force, halo, scale_low, minv, amat, norm_own, norm_prev, schur_prev,
    parts, picked, w_gap, w_fix, hot,
    in_sem, halo_send, halo_recv, init_send, init_recv, part_send, part_recv,
):
    n_grp, n_dom, planes, ny, nz, n_if = dims
    g, d = lax.axis_index("grp"), lax.axis_index("dom")
    n_dev = n_grp * n_dom
    me = g * n_dom + d
    n_pair = ny // WINDOW

    barrier = pltpu.get_barrier_semaphore()

    def greet(k, carry):
        to = lax.rem(me + k, n_dev)
        pl.semaphore_signal(
            barrier, inc=1, device_id=(to // n_dom, lax.rem(to, n_dom)), device_id_type=MESH
        )
        return carry

    sources = (disp, vel, ext_in, mass_in, scale_in, stiff_in, sub_in, own_in, peer_in, norm_in, schur_in)
    places = (o_u, o_v, ext, mass, scale, stiff, sub, own, peer, norm, schur)
    loads = [
        pltpu.make_async_copy(source, place, in_sem.at[k])
        for k, (source, place) in enumerate(zip(sources, places))
    ]
    for k in (5, 0, 3, 4, 9, 10, 1, 2, 6, 7, 8):
        loads[k].start()
    lax.fori_loop(1, n_dev, greet, 0)

    def rows_at(start, size):
        return pl.ds(pl.multiple_of(start, BLOCK), size)

    def after(q):
        return lax.rem(q + 1, n_pair)

    def before(q):
        return lax.rem(q + n_pair - 1, n_pair)

    def split_window(load, plane, q, odd):
        for comp in range(3):
            if odd:
                x = jnp.concatenate(
                    [load(comp, q * WINDOW + BLOCK), load(comp, after(q) * WINDOW)], 0
                )
            else:
                x = jnp.concatenate(
                    [load(comp, q * WINDOW), load(comp, q * WINDOW + BLOCK)], 0
                )
            for e in (0, 1):
                y = x if e == 0 else pltpu.roll(x, nz - 1, 1)
                high, low = halves(y)
                at = pl.ds(plane * IN_HALF + (comp * 2 + e) * WINDOW, WINDOW)
                lanes = slice(nz, 2 * nz) if odd else slice(0, nz)
                split_hi[q, at, lanes] = high
                split_lo[q, at, lanes] = low

    def own_rows(plane):
        return lambda comp, start: o_u[comp, rows_at(plane * ny + start, BLOCK), :]

    def halo_rows(slot, side):
        return lambda comp, start: halo[slot, side, comp, rows_at(start, BLOCK), :]

    @pl.when(d == 0)
    def _():
        scale_low[...] = jnp.zeros_like(scale_low)
        for slot in (0, 1):
            halo[slot, 0] = jnp.zeros((3, ny, nz), F32)

    @pl.when(d == n_dom - 1)
    def _():
        for slot in (0, 1):
            halo[slot, 1] = jnp.zeros((3, ny, nz), F32)

    def to_prev(slot, q):
        return pltpu.make_async_remote_copy(
            src_ref=o_u.at[:, rows_at(q * WINDOW, WINDOW), :],
            dst_ref=halo.at[slot, 1, :, rows_at(q * WINDOW, WINDOW), :],
            send_sem=halo_send.at[0, q],
            recv_sem=halo_recv.at[slot, 1, q],
            device_id=(g, d - 1),
            device_id_type=MESH,
        )

    def to_next(slot, q):
        return pltpu.make_async_remote_copy(
            src_ref=o_u.at[:, rows_at((planes - 1) * ny + q * WINDOW, WINDOW), :],
            dst_ref=halo.at[slot, 0, :, rows_at(q * WINDOW, WINDOW), :],
            send_sem=halo_send.at[1, q],
            recv_sem=halo_recv.at[slot, 0, q],
            device_id=(g, d + 1),
            device_id_type=MESH,
        )

    scale_copy = pltpu.make_async_remote_copy(
        src_ref=scale.at[pl.ds((planes - 1) * ny, ny), :],
        dst_ref=scale_low,
        send_sem=init_send.at[0],
        recv_sem=init_recv.at[0],
        device_id=(g, d + 1),
        device_id_type=MESH,
    )
    later = (lax.rem(g + 1, n_grp), d)
    norm_copy = pltpu.make_async_remote_copy(
        src_ref=norm_own,
        dst_ref=norm_prev,
        send_sem=init_send.at[1],
        recv_sem=init_recv.at[1],
        device_id=later,
        device_id_type=MESH,
    )
    schur_copy = pltpu.make_async_remote_copy(
        src_ref=schur,
        dst_ref=schur_prev,
        send_sem=init_send.at[2],
        recv_sem=init_recv.at[2],
        device_id=later,
        device_id_type=MESH,
    )

    loads[5].wait()
    high, low = halves(block_matrix(stiff[...]))
    amat[:, 0 : 2 * IN_HALF] = high
    amat[:, 2 * IN_HALF : 4 * IN_HALF] = high
    amat[:, 4 * IN_HALF : 6 * IN_HALF] = low
    for k in (0, 1, 2, 3, 4, 6, 7, 8, 9, 10):
        loads[k].wait()
    norm_own[...] = jnp.zeros_like(norm_own)
    for comp in range(3):
        norm_own[comp : comp + 1, 0:n_if] = norm[comp]
    minv[...] = 1.0 / mass[...]
    for plane in range(planes):
        for q in range(n_pair):
            for odd in (False, True):
                split_window(own_rows(plane), plane + 1, jnp.int32(q), odd)

    pl.semaphore_wait(barrier, n_dev - 1)

    for q in range(n_pair):
        @pl.when(d > 0)
        def _():
            to_prev(0, q).start()

        @pl.when(d < n_dom - 1)
        def _():
            to_next(0, q).start()
            if q == 1:
                scale_copy.start()

    norm_copy.start()
    schur_copy.start()

    two = 2 * n_if
    nodes = [own[0, i] for i in range(n_if)] + [peer[0, i] for i in range(n_if)]
    node_rows = [node // nz for node in nodes]

    def layer(index, corners, q, total):
        first = min(corners) * OUT_HALF
        weights = amat[first : first + len(corners) * OUT_HALF, :]
        rows_in = pl.ds(index * IN_HALF, 2 * IN_HALF)
        top = split_hi[q, rows_in, :]
        stacked = jnp.concatenate([top, split_lo[q, rows_in, :], top], 0)
        result = jnp.dot(weights, stacked, preferred_element_type=F32)
        for half in (0, 1):
            start = q * WINDOW + half * BLOCK
            if index == 0:
                factor = scale_low[rows_at(start, BLOCK), :]
            else:
                factor = scale[rows_at((index - 1) * ny + start, BLOCK), :]
            lanes = slice(half * nz, (half + 1) * nz)
            for k, a in enumerate(corners):
                for b in (0, 1):
                    for comp in range(3):
                        base = k * OUT_HALF + b * (OUT_HALF // 2) + comp * WINDOW
                        near = result[base : base + BLOCK, lanes] * factor
                        far = result[base + BLOCK : base + WINDOW, lanes] * factor
                        part = near + pltpu.roll(far, 1, 1)
                        key = (index - 1 + a, b, comp, half)
                        total[key] = total[key] + part if key in total else part

    count = jnp.full((1, nz), sub[0], jnp.int32)
    full_delta = coarse_step / count.astype(F32)

    def prepare():
        norm_copy.wait_recv()
        schur_copy.wait_recv()
        lane = iota((two, nz), 1)
        row = iota((two, nz), 0)
        columns = jnp.zeros((two, nz), jnp.int32)
        wide = iota((1, 3 * two), 1)
        rows = jnp.zeros((1, 3 * two), jnp.int32)
        for i in range(two):
            columns = jnp.where(row == i, nodes[i] - node_rows[i] * nz, columns)
            for rep in range(3):
                rows = jnp.where(wide == rep * two + i, node_rows[i], rows)
            picked[0, i : i + 1, :] = minv[pl.ds(node_rows[i], 1), :]
        at_node = lane == columns
        size = planes * ny
        hot[...] = (iota((size, 3 * two), 0) == rows).astype(F32).astype(BF16)
        inverse = picked[0]
        diagonal = iota((n_if, nz), 0) == iota((n_if, nz), 1)
        sign = jnp.where(row < n_if, -1.0, 1.0).astype(F32)
        for comp in range(3):
            cols = []
            for ref in (norm_own, norm_prev):
                spread = jnp.where(diagonal, ref[comp : comp + 1, :], 0.0)
                cols.append(jnp.sum(spread, axis=1, keepdims=True))
            here = jnp.where(at_node, jnp.concatenate(cols, 0), 0.0)
            w_gap[comp] = here
            w_fix[comp] = here * sign * inverse

    def advance(step, carry):
        slot = lax.rem(step, 2)
        delta = jnp.where(step < count, full_delta, 0.0)
        order = [lax.rem(step + i, n_pair) for i in range(n_pair)]

        def arrive(q):
            @pl.when(d > 0)
            def _():
                to_next(slot, q).wait_recv()

            @pl.when(d < n_dom - 1)
            def _():
                to_prev(slot, q).wait_recv()

        def update(q):
            @pl.when(d > 0)
            def _():
                to_prev(slot, q).wait_send()

            @pl.when(d < n_dom - 1)
            def _():
                to_next(slot, q).wait_send()

            for plane in range(planes):
                at = rows_at(plane * ny + q * WINDOW, WINDOW)
                last = rows_at(plane * ny + before(q) * WINDOW + BLOCK, BLOCK)
                for comp in range(3):
                    shifted = jnp.concatenate([force[1, comp, last, :], force[1, comp, at, :]], 0)
                    shifted = pltpu.roll(shifted, 1, 0)[BLOCK:]
                    inner = force[0, comp, at, :] + shifted
                    speed = o_v[comp, at, :] + delta * ((ext[comp, at, :] - inner) * minv[at, :])
                    o_v[comp, at, :] = speed
                    o_u[comp, at, :] = o_u[comp, at, :] + delta * speed

            @pl.when((step < MAXSUB - 1) & (d > 0))
            def _():
                to_prev(1 - slot, q).start()

            @pl.when((step < MAXSUB - 1) & (d < n_dom - 1))
            def _():
                to_next(1 - slot, q).start()

        def own_windows(q, odd):
            for plane in range(planes):
                split_window(own_rows(plane), plane + 1, q, odd)

        def halo_windows(q, odd):
            split_window(halo_rows(slot, 0), 0, q, odd)
            split_window(halo_rows(slot, 1), planes + 1, q, odd)

        for i, q in enumerate(order):
            total = {}
            for index in range(1, planes):
                layer(index, (0, 1), q, total)
            if i == 0:
                @pl.when((step == 0) & (d > 0))
                def _():
                    scale_copy.wait_recv()

                arrive(q)
                halo_windows(q, False)
            if i < n_pair - 1:
                arrive(order[i + 1])
                halo_windows(order[i + 1], False)
            halo_windows(q, True)
            layer(0, (1,), q, total)
            layer(planes, (0,), q, total)
            for (plane, b, comp, half), part in total.items():
                at = rows_at(plane * ny + q * WINDOW + half * BLOCK, BLOCK)
                force[b, comp, at, :] = part
            if i > 0:
                update(q)
                own_windows(q, False)
            if i > 1:
                own_windows(order[i - 1], True)
        update(order[0])
        own_windows(order[0], False)
        own_windows(order[0], True)
        own_windows(order[-1], True)

        @pl.when(step == 0)
        def _():
            prepare()

        return carry

    lax.fori_loop(0, MAXSUB, advance, 0)

    for comp in range(3):
        for i in range(two):
            picked[comp, i : i + 1, :] = o_v[comp, pl.ds(node_rows[i], 1), :]
    summed = picked[0] * w_gap[0] + picked[1] * w_gap[1] + picked[2] * w_gap[2]
    columns = jnp.sum(summed, axis=1, keepdims=True)
    per_row = nz // n_if
    offset = lax.rem(d, per_row) * n_if
    place = iota((n_if, nz), 1) == iota((n_if, nz), 0) + offset
    for k in (0, 1):
        spread = jnp.where(place, columns[k * n_if : (k + 1) * n_if, :], 0.0)
        parts[me, k : k + 1, :] = jnp.sum(spread, axis=0, keepdims=True)

    def part_copy(to, source):
        return pltpu.make_async_remote_copy(
            src_ref=parts.at[source],
            dst_ref=parts.at[source],
            send_sem=part_send.at[to],
            recv_sem=part_recv.at[source],
            device_id=(to // n_dom, lax.rem(to, n_dom)),
            device_id_type=MESH,
        )

    def send(k, carry):
        part_copy(lax.rem(me + k, n_dev), me).start()
        return carry

    def receive(k, carry):
        source = lax.rem(me + k, n_dev)
        part_copy(source, source).wait_recv()
        return carry

    def finish(k, carry):
        part_copy(lax.rem(me + k, n_dev), me).wait_send()
        return carry

    lax.fori_loop(1, n_dev, send, 0)
    lax.fori_loop(1, n_dev, receive, 0)

    n_rows = n_dom // per_row
    totals = [
        [
            jnp.sum(parts[group * n_dom + k * per_row : group * n_dom + (k + 1) * per_row], axis=0)
            for k in range(n_rows)
        ]
        for group in range(n_grp)
    ]
    mine = jnp.zeros((n_if, nz), F32)
    before = jnp.zeros((n_if, nz), F32)
    for group in range(n_grp):
        for k in range(n_rows):
            gap = totals[group][k][0:1] - totals[(group + 1) % n_grp][k][1:2]
            at = slice((group * n_rows + k) * nz, (group * n_rows + k + 1) * nz)
            mine = mine + schur[:, at] * gap
            before = before + schur_prev[:, at] * gap
    factors = jnp.sum(jnp.concatenate([mine, before], 0), axis=1, keepdims=True)
    fixes = jnp.concatenate([factors * w_fix[comp] for comp in range(3)], 1)
    first, rest = fixes.astype(BF16), fixes
    rest = rest - first.astype(F32)
    second = rest.astype(BF16)
    third = (rest - second.astype(F32)).astype(BF16)
    change = jnp.dot(
        hot[...], jnp.concatenate([first, second, third], 0), preferred_element_type=F32
    )
    for comp in range(3):
        o_v[comp] = o_v[comp] + change[:, comp * nz : (comp + 1) * nz]

    lax.fori_loop(1, n_dev, finish, 0)
    norm_copy.wait_send()
    schur_copy.wait_send()

    @pl.when(d < n_dom - 1)
    def _():
        scale_copy.wait_send()


def solution(mesh):
    n_grp, n_dom = mesh.shape["grp"], mesh.shape["dom"]

    def on_device(
        displacement, velocity, external, mass, elem_scale, stiffness,
        substeps, own_nodes, peer_nodes, normals, schur_inverse,
    ):
        _, _, planes, ny, nz = displacement.shape
        n_if = own_nodes.shape[1]
        n_dev = n_grp * n_dom
        n_lam = schur_inverse.shape[1]
        rows = planes * ny
        field = jax.ShapeDtypeStruct((3, rows, nz), F32)
        vmem = pl.BlockSpec(memory_space=pltpu.VMEM)
        new_u, new_v = pl.pallas_call(
            functools.partial(kernel, (n_grp, n_dom, planes, ny, nz, n_if)),
            out_shape=(field, field),
            in_specs=[pl.BlockSpec(memory_space=pltpu.HBM)] * 11,
            out_specs=(vmem, vmem),
            scratch_shapes=[
                pltpu.VMEM((3, rows, nz), F32),
                pltpu.VMEM((rows, nz), F32),
                pltpu.VMEM((rows, nz), F32),
                pltpu.VMEM((24, 24), F32),
                pltpu.SMEM((1,), jnp.int32),
                pltpu.SMEM((1, n_if), jnp.int32),
                pltpu.SMEM((1, n_if), jnp.int32),
                pltpu.VMEM((3, 1, n_if), F32),
                pltpu.VMEM((n_if, n_lam), F32),
                pltpu.VMEM((ny // WINDOW, (planes + 2) * IN_HALF, 2 * nz), BF16),
                pltpu.VMEM((ny // WINDOW, (planes + 2) * IN_HALF, 2 * nz), BF16),
                pltpu.VMEM((2, 3, rows, nz), F32),
                pltpu.VMEM((2, 2, 3, ny, nz), F32),
                pltpu.VMEM((ny, nz), F32),
                pltpu.VMEM((rows, nz), F32),
                pltpu.VMEM((2 * OUT_HALF, 6 * IN_HALF), BF16),
                pltpu.VMEM((8, nz), F32),
                pltpu.VMEM((8, nz), F32),
                pltpu.VMEM((n_if, n_lam), F32),
                pltpu.VMEM((n_dev, 2, nz), F32),
                pltpu.VMEM((3, 2 * n_if, nz), F32),
                pltpu.VMEM((3, 2 * n_if, nz), F32),
                pltpu.VMEM((3, 2 * n_if, nz), F32),
                pltpu.VMEM((rows, 6 * n_if), BF16),
                pltpu.SemaphoreType.DMA((11,)),
                pltpu.SemaphoreType.DMA((2, ny // WINDOW)),
                pltpu.SemaphoreType.DMA((2, 2, ny // WINDOW)),
                pltpu.SemaphoreType.DMA((3,)),
                pltpu.SemaphoreType.DMA((3,)),
                pltpu.SemaphoreType.DMA((n_dev,)),
                pltpu.SemaphoreType.DMA((n_dev,)),
            ],
            compiler_params=pltpu.CompilerParams(
                collective_id=0, has_side_effects=True, vmem_limit_bytes=67_043_328
            ),
        )(
            displacement.reshape(3, rows, nz),
            velocity.reshape(3, rows, nz),
            external.reshape(3, rows, nz),
            mass.reshape(rows, nz),
            elem_scale.reshape(rows, nz),
            stiffness[0],
            substeps,
            own_nodes,
            peer_nodes,
            jnp.transpose(normals, (1, 0, 2)),
            schur_inverse,
        )
        shape = displacement.shape
        return new_u.reshape(shape), new_v.reshape(shape)

    return jax.shard_map(
        on_device,
        mesh=mesh,
        in_specs=(
            P("grp", None, "dom", None, None),
            P("grp", None, "dom", None, None),
            P("grp", None, "dom", None, None),
            P("grp", "dom", None, None),
            P("grp", "dom", None, None),
            P("grp", None, None),
            P("grp"),
            P("grp", "dom"),
            P("grp", "dom"),
            P("grp", None, "dom"),
            P(("grp", "dom"), None),
        ),
        out_specs=(P("grp", None, "dom", None, None), P("grp", None, "dom", None, None)),
        check_vma=False,
    )
```

```python
import functools

import jax
import jax.numpy as jnp
from jax import lax
from jax.experimental import pallas as pl
from jax.experimental.pallas import tpu as pltpu
from jax.sharding import PartitionSpec as P

MAXSUB = 8
TURN = 4
MESH = pl.DeviceIdType.MESH
HIGH = lax.Precision.HIGHEST
F32 = jnp.float32
BF16 = jnp.bfloat16

coarse_step = 0.4

BLOCK = 8
WINDOW = 16
OUT_HALF = 12 * BLOCK
IN_HALF = 6 * WINDOW


def iota(shape, dim):
    return lax.broadcasted_iota(jnp.int32, shape, dim)


def halves(x):
    high = x.astype(BF16)
    return high, (x - high.astype(F32)).astype(BF16)


def block_matrix(kmat):
    outs, ins = 2 * OUT_HALF, 2 * IN_HALF

    def out_parts(q):
        a = (q >= OUT_HALF).astype(jnp.int32)
        q = q - a * OUT_HALF
        b = (q >= OUT_HALF // 2).astype(jnp.int32)
        q = q - b * (OUT_HALF // 2)
        return a, b, q >> 4, (q >> 3) & 1, q & 7

    def in_parts(q):
        a = (q >= IN_HALF).astype(jnp.int32)
        q = q - a * IN_HALF
        return a, q >> 5, (q >> 4) & 1, q & 15

    a, b, comp, e, _ = out_parts(iota((outs, 24), 0))
    pick = (iota((outs, 24), 1) == 3 * (4 * a + 2 * b + e) + comp).astype(F32)
    left = jnp.dot(pick, kmat, precision=HIGH, preferred_element_type=F32)
    row = out_parts(iota((outs, ins), 0))[4]
    window_row = in_parts(iota((outs, ins), 1))[3]
    total = jnp.zeros((outs, ins), F32)
    a, comp, e, _ = in_parts(iota((24, ins), 1))
    for b in (0, 1):
        place = (iota((24, ins), 0) == 3 * (4 * a + 2 * b + e) + comp).astype(F32)
        spread = jnp.dot(left, place, precision=HIGH, preferred_element_type=F32)
        total = jnp.where(window_row - row == b, spread, total)
    return total


def kernel(
    dims, disp, vel, ext_in, mass_in, scale_in, stiff_in, sub_in, own_in, peer_in, norm_in, schur_in,
    o_u, o_v,
    ext, mass, scale, stiff, sub, own, peer, norm, schur,
    split_hi, split_lo, force, halo, scale_low, minv, amat, norm_own, norm_prev, schur_prev,
    parts, picked, w_gap, w_fix, hot,
    in_sem, halo_send, halo_recv, init_send, init_recv, part_send, part_recv,
):
    n_grp, n_dom, planes, ny, nz, n_if = dims
    g, d = lax.axis_index("grp"), lax.axis_index("dom")
    n_dev = n_grp * n_dom
    me = g * n_dom + d
    n_pair = ny // WINDOW

    barrier = pltpu.get_barrier_semaphore()

    def greet(k, carry):
        to = lax.rem(me + k, n_dev)
        pl.semaphore_signal(
            barrier, inc=1, device_id=(to // n_dom, lax.rem(to, n_dom)), device_id_type=MESH
        )
        return carry

    sources = (disp, vel, ext_in, mass_in, scale_in, stiff_in, sub_in, own_in, peer_in, norm_in, schur_in)
    places = (o_u, o_v, ext, mass, scale, stiff, sub, own, peer, norm, schur)
    loads = [
        pltpu.make_async_copy(source, place, in_sem.at[k])
        for k, (source, place) in enumerate(zip(sources, places))
    ]
    for k in (5, 0, 3, 4, 9, 10, 1, 2, 6, 7, 8):
        loads[k].start()
    lax.fori_loop(1, n_dev, greet, 0)

    def rows_at(start, size):
        return pl.ds(start, size)

    def after(q):
        return (q + 1) % n_pair

    def before(q):
        return (q - 1) % n_pair

    def split_window(load, plane, q, odd):
        for comp in range(3):
            if odd:
                x = jnp.concatenate(
                    [load(comp, q * WINDOW + BLOCK), load(comp, after(q) * WINDOW)], 0
                )
            else:
                x = jnp.concatenate(
                    [load(comp, q * WINDOW), load(comp, q * WINDOW + BLOCK)], 0
                )
            for e in (0, 1):
                y = x if e == 0 else pltpu.roll(x, nz - 1, 1)
                high, low = halves(y)
                at = pl.ds(plane * IN_HALF + (comp * 2 + e) * WINDOW, WINDOW)
                lanes = slice(nz, 2 * nz) if odd else slice(0, nz)
                split_hi[q, at, lanes] = high
                split_lo[q, at, lanes] = low

    def own_rows(plane):
        return lambda comp, start: o_u[comp, rows_at(plane * ny + start, BLOCK), :]

    def halo_rows(slot, side):
        return lambda comp, start: halo[slot, side, comp, rows_at(start, BLOCK), :]

    @pl.when(d == 0)
    def _():
        scale_low[...] = jnp.zeros_like(scale_low)
        for slot in (0, 1):
            halo[slot, 0] = jnp.zeros((3, ny, nz), F32)

    @pl.when(d == n_dom - 1)
    def _():
        for slot in (0, 1):
            halo[slot, 1] = jnp.zeros((3, ny, nz), F32)

    def to_prev(slot, q):
        return pltpu.make_async_remote_copy(
            src_ref=o_u.at[:, rows_at(q * WINDOW, WINDOW), :],
            dst_ref=halo.at[slot, 1, :, rows_at(q * WINDOW, WINDOW), :],
            send_sem=halo_send.at[0, q],
            recv_sem=halo_recv.at[slot, 1, q],
            device_id=(g, d - 1),
            device_id_type=MESH,
        )

    def to_next(slot, q):
        return pltpu.make_async_remote_copy(
            src_ref=o_u.at[:, rows_at((planes - 1) * ny + q * WINDOW, WINDOW), :],
            dst_ref=halo.at[slot, 0, :, rows_at(q * WINDOW, WINDOW), :],
            send_sem=halo_send.at[1, q],
            recv_sem=halo_recv.at[slot, 0, q],
            device_id=(g, d + 1),
            device_id_type=MESH,
        )

    scale_copy = pltpu.make_async_remote_copy(
        src_ref=scale.at[pl.ds((planes - 1) * ny, ny), :],
        dst_ref=scale_low,
        send_sem=init_send.at[0],
        recv_sem=init_recv.at[0],
        device_id=(g, d + 1),
        device_id_type=MESH,
    )
    later = (lax.rem(g + 1, n_grp), d)
    norm_copy = pltpu.make_async_remote_copy(
        src_ref=norm_own,
        dst_ref=norm_prev,
        send_sem=init_send.at[1],
        recv_sem=init_recv.at[1],
        device_id=later,
        device_id_type=MESH,
    )
    schur_copy = pltpu.make_async_remote_copy(
        src_ref=schur,
        dst_ref=schur_prev,
        send_sem=init_send.at[2],
        recv_sem=init_recv.at[2],
        device_id=later,
        device_id_type=MESH,
    )

    loads[5].wait()
    high, low = halves(block_matrix(stiff[...]))
    amat[:, 0 : 2 * IN_HALF] = high
    amat[:, 2 * IN_HALF : 4 * IN_HALF] = high
    amat[:, 4 * IN_HALF : 6 * IN_HALF] = low
    for k in (0, 1, 2, 3, 4, 6, 7, 8, 9, 10):
        loads[k].wait()
    norm_own[...] = jnp.zeros_like(norm_own)
    for comp in range(3):
        norm_own[comp : comp + 1, 0:n_if] = norm[comp]
    minv[...] = 1.0 / mass[...]
    for plane in range(planes):
        for q in range(n_pair):
            for odd in (False, True):
                split_window(own_rows(plane), plane + 1, q, odd)

    pl.semaphore_wait(barrier, n_dev - 1)

    for q in range(n_pair):
        @pl.when(d > 0)
        def _():
            to_prev(0, q).start()

        @pl.when(d < n_dom - 1)
        def _():
            to_next(0, q).start()
            if q == 1:
                scale_copy.start()

    norm_copy.start()
    schur_copy.start()

    two = 2 * n_if
    nodes = [own[0, i] for i in range(n_if)] + [peer[0, i] for i in range(n_if)]
    node_rows = [node // nz for node in nodes]

    def layer(index, corners, q, seen):
        first = min(corners) * OUT_HALF
        weights = amat[first : first + len(corners) * OUT_HALF, :]
        rows_in = pl.ds(index * IN_HALF, 2 * IN_HALF)
        top = split_hi[q, rows_in, :]
        stacked = jnp.concatenate([top, split_lo[q, rows_in, :], top], 0)
        result = jnp.dot(weights, stacked, preferred_element_type=F32)
        for half in (0, 1):
            start = q * WINDOW + half * BLOCK
            if index == 0:
                factor = scale_low[rows_at(start, BLOCK), :]
            else:
                factor = scale[rows_at((index - 1) * ny + start, BLOCK), :]
            lanes = slice(half * nz, (half + 1) * nz)
            for k, a in enumerate(corners):
                at = rows_at((index - 1 + a) * ny + start, BLOCK)
                for b in (0, 1):
                    for comp in range(3):
                        base = k * OUT_HALF + b * (OUT_HALF // 2) + comp * WINDOW
                        near = result[base : base + BLOCK, lanes] * factor
                        far = result[base + BLOCK : base + WINDOW, lanes] * factor
                        part = near + pltpu.roll(far, 1, 1)
                        if index - 1 + a in seen:
                            part = part + force[b, comp, at, :]
                        force[b, comp, at, :] = part

    count = jnp.full((1, nz), sub[0], jnp.int32)
    full_delta = coarse_step / count.astype(F32)

    def prepare():
        norm_copy.wait_recv()
        schur_copy.wait_recv()
        lane = iota((two, nz), 1)
        row = iota((two, nz), 0)
        columns = jnp.zeros((two, nz), jnp.int32)
        wide = iota((1, 3 * two), 1)
        rows = jnp.zeros((1, 3 * two), jnp.int32)
        for i in range(two):
            columns = jnp.where(row == i, nodes[i] - node_rows[i] * nz, columns)
            for rep in range(3):
                rows = jnp.where(wide == rep * two + i, node_rows[i], rows)
            picked[0, i : i + 1, :] = minv[pl.ds(node_rows[i], 1), :]
        at_node = lane == columns
        size = planes * ny
        hot[...] = (iota((size, 3 * two), 0) == rows).astype(F32).astype(BF16)
        inverse = picked[0]
        diagonal = iota((n_if, nz), 0) == iota((n_if, nz), 1)
        sign = jnp.where(row < n_if, -1.0, 1.0).astype(F32)
        for comp in range(3):
            cols = []
            for ref in (norm_own, norm_prev):
                spread = jnp.where(diagonal, ref[comp : comp + 1, :], 0.0)
                cols.append(jnp.sum(spread, axis=1, keepdims=True))
            here = jnp.where(at_node, jnp.concatenate(cols, 0), 0.0)
            w_gap[comp] = here
            w_fix[comp] = here * sign * inverse

    def advance(turn, carry):
        for part in range(TURN):
            one_step(turn, part)
        return carry

    def one_step(turn, part):
        slot = part % 2
        delta = jnp.where(turn * TURN + part < count, full_delta, 0.0)
        order = [(part + i) % n_pair for i in range(n_pair)]
        more = True if part < TURN - 1 else turn < MAXSUB // TURN - 1

        def arrive(*pairs):
            @pl.when(d > 0)
            def _():
                for q in pairs:
                    to_next(slot, q).wait_recv()

            @pl.when(d < n_dom - 1)
            def _():
                for q in pairs:
                    to_prev(slot, q).wait_recv()

        def sent():
            @pl.when(d > 0)
            def _():
                for q in order:
                    to_prev(slot, q).wait_send()

            @pl.when(d < n_dom - 1)
            def _():
                for q in order:
                    to_next(slot, q).wait_send()

        def update(q):
            for plane in range(planes):
                at = rows_at(plane * ny + q * WINDOW, WINDOW)
                last = rows_at(plane * ny + before(q) * WINDOW + BLOCK, BLOCK)
                for comp in range(3):
                    shifted = jnp.concatenate([force[1, comp, last, :], force[1, comp, at, :]], 0)
                    shifted = pltpu.roll(shifted, 1, 0)[BLOCK:]
                    inner = force[0, comp, at, :] + shifted
                    speed = o_v[comp, at, :] + delta * ((ext[comp, at, :] - inner) * minv[at, :])
                    o_v[comp, at, :] = speed
                    o_u[comp, at, :] = o_u[comp, at, :] + delta * speed

            @pl.when((d > 0) & more)
            def _():
                to_prev(1 - slot, q).start()

            @pl.when((d < n_dom - 1) & more)
            def _():
                to_next(1 - slot, q).start()

        def own_windows(q, odd):
            for plane in range(planes):
                split_window(own_rows(plane), plane + 1, q, odd)

        def halo_windows(q, odd):
            split_window(halo_rows(slot, 0), 0, q, odd)
            split_window(halo_rows(slot, 1), planes + 1, q, odd)

        seen = set()
        for index in range(1, planes):
            for q in order:
                layer(index, (0, 1), q, seen)
            seen.update((index - 1, index))
        for i, q in enumerate(order):
            if i == 0:
                if part == 0:
                    @pl.when((turn == 0) & (d > 0))
                    def _():
                        scale_copy.wait_recv()

                arrive(q, order[1])
                sent()
                halo_windows(q, False)
            elif i < n_pair - 1:
                arrive(order[i + 1])
            if i < n_pair - 1:
                halo_windows(order[i + 1], False)
            halo_windows(q, True)
            fresh = set(seen)
            layer(0, (1,), q, fresh)
            fresh.add(0)
            layer(planes, (0,), q, fresh)
            if i > 0:
                update(q)
                own_windows(q, False)
            if i > 1:
                own_windows(order[i - 1], True)
        update(order[0])
        own_windows(order[0], False)
        own_windows(order[0], True)
        own_windows(order[-1], True)

        if part == 0:
            @pl.when(turn == 0)
            def _():
                prepare()

    lax.fori_loop(0, MAXSUB // TURN, advance, 0)

    for comp in range(3):
        for i in range(two):
            picked[comp, i : i + 1, :] = o_v[comp, pl.ds(node_rows[i], 1), :]
    summed = picked[0] * w_gap[0] + picked[1] * w_gap[1] + picked[2] * w_gap[2]
    columns = jnp.sum(summed, axis=1, keepdims=True)
    per_row = nz // n_if
    offset = lax.rem(d, per_row) * n_if
    place = iota((n_if, nz), 1) == iota((n_if, nz), 0) + offset
    for k in (0, 1):
        spread = jnp.where(place, columns[k * n_if : (k + 1) * n_if, :], 0.0)
        parts[me, k : k + 1, :] = jnp.sum(spread, axis=0, keepdims=True)

    def part_copy(to, source):
        return pltpu.make_async_remote_copy(
            src_ref=parts.at[source],
            dst_ref=parts.at[source],
            send_sem=part_send.at[to],
            recv_sem=part_recv.at[source],
            device_id=(to // n_dom, lax.rem(to, n_dom)),
            device_id_type=MESH,
        )

    def send(k, carry):
        part_copy(lax.rem(me + k, n_dev), me).start()
        return carry

    def receive(k, carry):
        source = lax.rem(me + k, n_dev)
        part_copy(source, source).wait_recv()
        return carry

    def finish(k, carry):
        part_copy(lax.rem(me + k, n_dev), me).wait_send()
        return carry

    lax.fori_loop(1, n_dev, send, 0)
    lax.fori_loop(1, n_dev, receive, 0)

    n_rows = n_dom // per_row
    totals = [
        [
            jnp.sum(parts[group * n_dom + k * per_row : group * n_dom + (k + 1) * per_row], axis=0)
            for k in range(n_rows)
        ]
        for group in range(n_grp)
    ]
    mine = jnp.zeros((n_if, nz), F32)
    before = jnp.zeros((n_if, nz), F32)
    for group in range(n_grp):
        for k in range(n_rows):
            gap = totals[group][k][0:1] - totals[(group + 1) % n_grp][k][1:2]
            at = slice((group * n_rows + k) * nz, (group * n_rows + k + 1) * nz)
            mine = mine + schur[:, at] * gap
            before = before + schur_prev[:, at] * gap
    factors = jnp.sum(jnp.concatenate([mine, before], 0), axis=1, keepdims=True)
    fixes = jnp.concatenate([factors * w_fix[comp] for comp in range(3)], 1)
    first, rest = fixes.astype(BF16), fixes
    rest = rest - first.astype(F32)
    second = rest.astype(BF16)
    third = (rest - second.astype(F32)).astype(BF16)
    change = jnp.dot(
        hot[...], jnp.concatenate([first, second, third], 0), preferred_element_type=F32
    )
    for comp in range(3):
        o_v[comp] = o_v[comp] + change[:, comp * nz : (comp + 1) * nz]

    lax.fori_loop(1, n_dev, finish, 0)
    norm_copy.wait_send()
    schur_copy.wait_send()

    @pl.when(d < n_dom - 1)
    def _():
        scale_copy.wait_send()


def solution(mesh):
    n_grp, n_dom = mesh.shape["grp"], mesh.shape["dom"]

    def on_device(
        displacement, velocity, external, mass, elem_scale, stiffness,
        substeps, own_nodes, peer_nodes, normals, schur_inverse,
    ):
        _, _, planes, ny, nz = displacement.shape
        n_if = own_nodes.shape[1]
        n_dev = n_grp * n_dom
        n_lam = schur_inverse.shape[1]
        rows = planes * ny
        field = jax.ShapeDtypeStruct((3, rows, nz), F32)
        vmem = pl.BlockSpec(memory_space=pltpu.VMEM)
        new_u, new_v = pl.pallas_call(
            functools.partial(kernel, (n_grp, n_dom, planes, ny, nz, n_if)),
            out_shape=(field, field),
            in_specs=[pl.BlockSpec(memory_space=pltpu.HBM)] * 11,
            out_specs=(vmem, vmem),
            scratch_shapes=[
                pltpu.VMEM((3, rows, nz), F32),
                pltpu.VMEM((rows, nz), F32),
                pltpu.VMEM((rows, nz), F32),
                pltpu.VMEM((24, 24), F32),
                pltpu.SMEM((1,), jnp.int32),
                pltpu.SMEM((1, n_if), jnp.int32),
                pltpu.SMEM((1, n_if), jnp.int32),
                pltpu.VMEM((3, 1, n_if), F32),
                pltpu.VMEM((n_if, n_lam), F32),
                pltpu.VMEM((ny // WINDOW, (planes + 2) * IN_HALF, 2 * nz), BF16),
                pltpu.VMEM((ny // WINDOW, (planes + 2) * IN_HALF, 2 * nz), BF16),
                pltpu.VMEM((2, 3, rows, nz), F32),
                pltpu.VMEM((2, 2, 3, ny, nz), F32),
                pltpu.VMEM((ny, nz), F32),
                pltpu.VMEM((rows, nz), F32),
                pltpu.VMEM((2 * OUT_HALF, 6 * IN_HALF), BF16),
                pltpu.VMEM((8, nz), F32),
                pltpu.VMEM((8, nz), F32),
                pltpu.VMEM((n_if, n_lam), F32),
                pltpu.VMEM((n_dev, 2, nz), F32),
                pltpu.VMEM((3, 2 * n_if, nz), F32),
                pltpu.VMEM((3, 2 * n_if, nz), F32),
                pltpu.VMEM((3, 2 * n_if, nz), F32),
                pltpu.VMEM((rows, 6 * n_if), BF16),
                pltpu.SemaphoreType.DMA((11,)),
                pltpu.SemaphoreType.DMA((2, ny // WINDOW)),
                pltpu.SemaphoreType.DMA((2, 2, ny // WINDOW)),
                pltpu.SemaphoreType.DMA((3,)),
                pltpu.SemaphoreType.DMA((3,)),
                pltpu.SemaphoreType.DMA((n_dev,)),
                pltpu.SemaphoreType.DMA((n_dev,)),
            ],
            compiler_params=pltpu.CompilerParams(
                collective_id=0, has_side_effects=True, vmem_limit_bytes=67_043_328
            ),
        )(
            displacement.reshape(3, rows, nz),
            velocity.reshape(3, rows, nz),
            external.reshape(3, rows, nz),
            mass.reshape(rows, nz),
            elem_scale.reshape(rows, nz),
            stiffness[0],
            substeps,
            own_nodes,
            peer_nodes,
            jnp.transpose(normals, (1, 0, 2)),
            schur_inverse,
        )
        shape = displacement.shape
        return new_u.reshape(shape), new_v.reshape(shape)

    return jax.shard_map(
        on_device,
        mesh=mesh,
        in_specs=(
            P("grp", None, "dom", None, None),
            P("grp", None, "dom", None, None),
            P("grp", None, "dom", None, None),
            P("grp", "dom", None, None),
            P("grp", "dom", None, None),
            P("grp", None, None),
            P("grp"),
            P("grp", "dom"),
            P("grp", "dom"),
            P("grp", None, "dom"),
            P(("grp", "dom"), None),
        ),
        out_specs=(P("grp", None, "dom", None, None), P("grp", None, "dom", None, None)),
        check_vma=False,
    )
```
